32 devices in a mesh: energy: 8 (over z, y), cell: 4 (over x, core).
Axes of the slice: x: 2, y: 2, z: 4, core: 2. Of those that a mesh axis runs over, the one named last changes fastest.
Arguments:
- g_lesser: float32 [2, 8, 4, 256, 256], P(None, 'energy', 'cell'), may hold values from -6 to 6
- g_greater: float32 [2, 8, 4, 256, 256], P(None, 'energy', 'cell'), may hold values from -6 to 6
- w_diag: float32 [2, 8, 4, 256, 256], P(None, 'energy', 'cell'), may hold values from -0.25 to 0.25
- w_upper: float32 [2, 8, 4, 256, 256], P(None, 'energy', 'cell'), may hold values from -0.25 to 0.25
- coupled: int32 [4], P('cell'), may hold values from 1 to 16
Outputs:
- polarization: float32 [2, 8, 4, 256, 256], P(None, 'energy', 'cell')
- screened: float32 [2, 8, 4, 256, 256], P(None, 'energy', 'cell')
The draws below stay inside these ranges and needn't reach their ends.
All inputs are finite; a program needn't handle non-finite values.
Results may differ from the reference program's by a relative error of at most 0.0003.
Values sent between devices are 32-bit elements; how exact they have to be, the bound alone decides.
A program may use at most 64 MiB of HBM per device.

```python
import jax
import jax.numpy as jnp
from jax import lax

B = 256
NE = 8
NC = 4


def set_ends(values, stream_key, least, top_value):
    dims = values.shape
    spot = [jax.random.randint(jax.random.fold_in(stream_key, axis), (), 0, dims[axis]) for axis in range(len(dims))]
    values = values.at[tuple(spot)].set(least)
    longest = dims.index(max(dims))
    spot[longest] = (spot[longest] + 1) % dims[longest]
    return values.at[tuple(spot)].set(top_value)


def block_scale(rng, shape, pieces, smallest, high):
    gain = 1.0
    for axis_at, parts in pieces:
        draws = jax.random.uniform(jax.random.fold_in(jax.random.fold_in(rng, 6), axis_at), (parts,), jnp.float32, smallest / len(pieces), high / len(pieces))
        gain = gain * jnp.repeat(jnp.exp(draws), shape[axis_at] // parts).reshape((-1,) + (1,) * (len(shape) - 1 - axis_at))
    return gain


def gaussian(own_key, dims, deviation, most, shards=(), kind=jnp.bfloat16):
    array = deviation * jax.random.normal(own_key, dims, jnp.float32)
    if shards:
        array = array * block_scale(own_key, dims, shards, -0.22, 0.18)
    return jnp.clip(array, -most, most).astype(kind)


def setup_inputs(seed: int = 0) -> dict:
    key_of = jax.random.split(jax.random.key(seed), 6)
    g_lesser = gaussian(key_of[0], (2, NE, NC, B, B), 1.0, 6.0, ((1, 8), (2, 4)), jnp.float32)
    g_greater = gaussian(key_of[1], (2, NE, NC, B, B), 1.0, 6.0, ((1, 8), (2, 4)), jnp.float32)
    w_diag = gaussian(key_of[2], (2, NE, NC, B, B), (2 * B) ** -0.5, 0.25, ((1, 8), (2, 4)), jnp.float32)
    w_upper = gaussian(key_of[3], (2, NE, NC, B, B), (2 * B) ** -0.5, 0.25, ((1, 8), (2, 4)), jnp.float32)
    coupled = set_ends(jax.random.randint(key_of[4], (NC,), 1, 17), jax.random.fold_in(key_of[4], 1), 1, 16).astype(jnp.int32)
    return dict(g_lesser=g_lesser, g_greater=g_greater, w_diag=w_diag, w_upper=w_upper, coupled=coupled)


def complex_product(left, right):

    def matmul(first, second):
        return jnp.einsum('...ij,...jk->...ik', first, second, precision=lax.Precision.HIGHEST)
    real = matmul(left[0], right[0]) - matmul(left[1], right[1])
    imaginary = matmul(left[0], right[1]) + matmul(left[1], right[0])
    return jnp.stack([real, imaginary])

def adjoint(block):
    return jnp.stack([jnp.swapaxes(block[0], -1, -2), -jnp.swapaxes(block[1], -1, -2)])

def transposed(block):
    return jnp.stack([jnp.swapaxes(block[0], -1, -2), jnp.swapaxes(block[1], -1, -2)])

def conjugate(block):
    return jnp.stack([block[0], -block[1]])

def reference(g_lesser, g_greater, w_diag, w_upper, coupled):
    greater_t = jnp.swapaxes(g_greater, 3, 4)
    padded = jnp.concatenate([jnp.zeros_like(greater_t), greater_t], axis=1)

    def polar_at(omega):
        start = (NE - omega).astype(jnp.int32)
        shifted = lax.dynamic_slice_in_dim(padded, start, NE, axis=1)
        real = lax.optimization_barrier(jnp.sum(g_lesser[0] * shifted[0] - g_lesser[1] * shifted[1], axis=0))
        imaginary = lax.optimization_barrier(jnp.sum(g_lesser[0] * shifted[1] + g_lesser[1] * shifted[0], axis=0))
        return jnp.stack([imaginary, -real]) / jnp.sqrt(jnp.float32(NE))
    stacked = lax.map(polar_at, jnp.arange(NE, dtype=jnp.int32))
    polarization = jnp.moveaxis(stacked, 0, 1)
    coupling = (coupled.astype(g_lesser.dtype) * 0.125)[None, None, :, None, None]
    upper_block = w_upper * coupling
    zero_cell = jnp.zeros_like(polarization[:, :, :1])
    next_polar = jnp.concatenate([polarization[:, :, 1:], zero_cell], axis=2)
    prev_polar = jnp.concatenate([zero_cell, polarization[:, :, :-1]], axis=2)
    prev_upper = jnp.concatenate([jnp.zeros_like(upper_block[:, :, :1]), upper_block[:, :, :-1]], axis=2)
    own_term = complex_product(complex_product(w_diag, polarization), adjoint(w_diag))
    upper_term = complex_product(complex_product(upper_block, next_polar), adjoint(upper_block))
    lower_term = complex_product(complex_product(transposed(prev_upper), prev_polar), conjugate(prev_upper))
    return (polarization, own_term + upper_term + lower_term)
```

```python
import functools
import math

import jax
import jax.numpy as jnp
from jax import lax
from jax.experimental import pallas as pl
from jax.experimental.pallas import tpu as pltpu
from jax.sharding import PartitionSpec as P

MESH = pl.DeviceIdType.MESH
F32 = jnp.float32
BF16 = jnp.bfloat16


def split(value):
    high = value.astype(BF16)
    return high, (value - high.astype(F32)).astype(BF16)


def product(left, right):
    total = jnp.dot(left[0], right[0], preferred_element_type=F32)
    total += jnp.dot(left[0], right[1], preferred_element_type=F32)
    total += jnp.dot(left[1], right[0], preferred_element_type=F32)
    return total


def kernel(
    n, nc, chunks,
    s_ref, l_ref, g_ref, d_hbm, u_hbm,
    pol_ref, scr_ref,
    gt, lbuf, gbuf, pout, pin, pbuf, pnext, pprev, dbuf, ubuf, uprev, parts,
    l_send, l_recv, g_send, g_recv, p_send, p_recv, c_send, c_recv, u_send, u_recv, in_sem, out_sem,
):
    me = lax.axis_index("energy")
    cell = lax.axis_index("cell")
    size = l_ref.shape[1]
    q4 = n // 4
    quarter, j = me // q4, me % q4
    third = (quarter // 2) * (1 - quarter % 2)
    fourth = (quarter // 2) * (quarter % 2)
    span = size // chunks
    rc = span // q4

    load_d = pltpu.make_async_copy(d_hbm, dbuf, in_sem.at[0])
    load_u = pltpu.make_async_copy(u_hbm, ubuf, in_sem.at[1])
    load_d.start()
    load_u.start()

    barrier = pltpu.get_barrier_semaphore()

    def greet(i, _):
        pl.semaphore_signal(barrier, inc=1, device_id=((me + i) % n, cell), device_id_type=MESH)
        return 0

    lax.fori_loop(1, n, greet, 0)

    @pl.when(cell > 0)
    def _():
        pl.semaphore_signal(barrier, inc=1, device_id=(me, cell - 1), device_id_type=MESH)

    @pl.when(cell < nc - 1)
    def _():
        pl.semaphore_signal(barrier, inc=1, device_id=(me, cell + 1), device_id_type=MESH)

    for part in range(2):
        gt[part] = g_ref[part].T

    pl.semaphore_wait(barrier, n - 1 + jnp.minimum(cell, 1) + jnp.minimum(nc - 1 - cell, 1))

    def near(k):
        return pl.ds(k * rc, rc)

    def far(k, row_owner):
        return pl.ds(pl.multiple_of(k * span + row_owner * rc, 8), rc)

    def l_copy(k, to):
        return pltpu.make_async_remote_copy(
            src_ref=l_ref.at[:, far(k, to)],
            dst_ref=lbuf.at[fourth * q4 + j, :, near(k)],
            send_sem=l_send.at[k, to],
            recv_sem=l_recv.at[k, fourth * q4 + j],
            device_id=((quarter - fourth) * q4 + to, cell),
            device_id_type=MESH,
        )

    def g_copy(k, step, to):
        return pltpu.make_async_remote_copy(
            src_ref=gt.at[:, far(k, to)],
            dst_ref=gbuf.at[me, :, near(k)],
            send_sem=g_send.at[k, step, to],
            recv_sem=g_recv.at[k, me],
            device_id=((quarter + step - fourth) * q4 + to, cell),
            device_id_type=MESH,
        )

    def p_copy(k, w):
        return pltpu.make_async_remote_copy(
            src_ref=pout.at[w, :, near(k)],
            dst_ref=pin.at[quarter, :, far(k, j)],
            send_sem=p_send.at[k, w],
            recv_sem=p_recv.at[k, quarter, j],
            device_id=(w, cell),
            device_id_type=MESH,
        )

    def landed(ref, sem):
        pltpu.make_async_copy(ref, ref, sem).wait()

    g_steps = (3 - quarter) * (1 - quarter // 2) + third + fourth

    for k in range(chunks):

        def send_g(i, _, k=k):
            step, to = g_steps - 1 - i // q4, (j + i) % q4

            @pl.when((quarter + step - fourth) * q4 + to != me)
            def _():
                g_copy(k, step, to).start()

            return 0

        lax.fori_loop(0, g_steps * q4, send_g, 0)

        def send_l(i, _, k=k):
            to = (j + i) % q4

            @pl.when((quarter - fourth) * q4 + to != me)
            def _():
                l_copy(k, to).start()

            return 0

        lax.fori_loop(0, q4, send_l, 0)

    @pl.when(quarter < 3)
    def _():
        for k in range(chunks):
            lbuf[j, :, near(k)] = l_ref[:, far(k, j)]
            gbuf[me, :, near(k)] = gt[:, far(k, j)]

    load_u.wait()
    ubuf[...] = ubuf[...] * (s_ref[0].astype(F32) * 0.125)

    def u_copy():
        return pltpu.make_async_remote_copy(
            src_ref=ubuf, dst_ref=uprev, send_sem=u_send, recv_sem=u_recv,
            device_id=(me, cell + 1), device_id_type=MESH,
        )

    load_d.wait()

    def prepare(slot, ref, turn):
        for part in range(2):
            value = ref[part]
            flipped = value.T
            forward = flipped if turn else value
            backward = value if turn else flipped
            parts[slot, part, 0], parts[slot, part, 1] = split(forward)
            parts[slot, 2 + part, 0], parts[slot, 2 + part, 1] = split(backward)

    prepare(0, dbuf, False)
    prepare(1, ubuf, False)

    @pl.when(cell < nc - 1)
    def _():
        u_copy().start()

    factor = 1.0 / math.sqrt(n)
    depth = q4 * (1 + third) * (1 - fourth)
    shifts = q4 * ((quarter + 1) * (1 - quarter // 2) + 4 * third)

    def compute(k):
        def wait_l(s, _):
            @pl.when(s != j)
            def _():
                landed(lbuf.at[s, :, near(k)], l_recv.at[k, s])

            return 0

        def wait_g(e, _):
            @pl.when(e != me)
            def _():
                landed(gbuf.at[e, :, near(k)], g_recv.at[k, e])

            return 0

        lax.fori_loop(0, depth, wait_l, 0)
        lax.fori_loop(0, shifts, wait_g, 0)

        def one_shift(w, _):
            def add(s, total):
                real, imaginary = total
                e = quarter * q4 + s - w
                lr, li = lbuf[s, 0, near(k)], lbuf[s, 1, near(k)]
                gr, gi = gbuf[e, 0, near(k)], gbuf[e, 1, near(k)]
                return real + (lr * gr - li * gi), imaginary + (lr * gi + li * gr)

            zero = jnp.zeros((rc, size), F32)
            first = jnp.maximum(w - quarter * q4, 0)
            real, imaginary = lax.fori_loop(first, depth, add, (zero, zero))
            pout[w, 0, near(k)] = imaginary * factor
            pout[w, 1, near(k)] = real * (-factor)
            return 0

        lax.fori_loop(0, shifts, one_shift, 0)

        def send_p(w, _):
            @pl.when(w != me)
            def _():
                p_copy(k, w).start()

            @pl.when(w == me)
            def _():
                pin[quarter, :, far(k, j)] = pout[w, :, near(k)]

            return 0

        lax.fori_loop(0, shifts, send_p, 0)

    def neighbour_copy(k, side):
        rows = pl.ds(k * span, span)
        return pltpu.make_async_remote_copy(
            src_ref=pbuf.at[:, rows],
            dst_ref=(pnext if side == 0 else pprev).at[:, rows],
            send_sem=c_send.at[k, side],
            recv_sem=c_recv.at[k, side],
            device_id=(me, cell - 1 if side == 0 else cell + 1),
            device_id_type=MESH,
        )

    def finish(k):
        rows = pl.ds(k * span, span)

        def wait_from(source):
            def wait_p(i, _):
                @pl.when(source * q4 + i != me)
                def _():
                    landed(pin.at[source, :, far(k, i)], p_recv.at[k, source, i])

                return 0

            lax.fori_loop(0, q4, wait_p, 0)

        @pl.when(quarter == 0)
        def _():
            wait_from(0)

        @pl.when(quarter <= 1)
        def _():
            wait_from(1)

        wait_from(2)

        @pl.when(quarter == 0)
        def _():
            pbuf[:, rows] = pin[0, :, rows] + pin[1, :, rows] + pin[2, :, rows]

        @pl.when(quarter == 1)
        def _():
            pbuf[:, rows] = pin[1, :, rows] + pin[2, :, rows]

        @pl.when(quarter >= 2)
        def _():
            pbuf[:, rows] = pin[2, :, rows]

        @pl.when(cell > 0)
        def _():
            neighbour_copy(k, 0).start()

        @pl.when(cell < nc - 1)
        def _():
            neighbour_copy(k, 1).start()

        pltpu.make_async_copy(pbuf.at[:, rows], pol_ref.at[:, rows], out_sem.at[k]).start()

    for k in range(chunks):
        compute(k)
        if k == 0:

            @pl.when(cell > 0)
            def _():
                landed(uprev, u_recv)
                prepare(2, uprev, True)

        if k > 0:
            finish(k - 1)
    finish(chunks - 1)

    def term(slot, ref):
        def pair(part):
            return parts[slot, part, 0], parts[slot, part, 1]

        p_real, p_imag = split(ref[0]), split(ref[1])
        mid_real = split(product(pair(0), p_real) - product(pair(1), p_imag))
        mid_imag = split(product(pair(0), p_imag) + product(pair(1), p_real))
        real = product(mid_real, pair(2)) + product(mid_imag, pair(3))
        imaginary = product(mid_imag, pair(2)) - product(mid_real, pair(3))
        return real, imaginary

    scr_ref[0], scr_ref[1] = term(0, pbuf)

    @pl.when(cell < nc - 1)
    def _():
        for k in range(chunks):
            landed(pnext.at[:, pl.ds(k * span, span)], c_recv.at[k, 0])
        real, imaginary = term(1, pnext)
        scr_ref[0] += real
        scr_ref[1] += imaginary

    @pl.when(cell > 0)
    def _():
        for k in range(chunks):
            landed(pprev.at[:, pl.ds(k * span, span)], c_recv.at[k, 1])
        real, imaginary = term(2, pprev)
        scr_ref[0] += real
        scr_ref[1] += imaginary

    for k in range(chunks):
        rows = pl.ds(k * span, span)

        def end_g(i, _, k=k):
            step, to = i // q4, i % q4

            @pl.when((quarter + step - fourth) * q4 + to != me)
            def _():
                g_copy(k, step, to).wait_send()

            return 0

        lax.fori_loop(0, g_steps * q4, end_g, 0)

        def end_l(to, _, k=k):
            @pl.when((quarter - fourth) * q4 + to != me)
            def _():
                l_copy(k, to).wait_send()

            return 0

        lax.fori_loop(0, q4, end_l, 0)

        def end_p(w, _, k=k):
            @pl.when(w != me)
            def _():
                p_copy(k, w).wait_send()

            return 0

        lax.fori_loop(0, shifts, end_p, 0)

        @pl.when(cell > 0)
        def _():
            neighbour_copy(k, 0).wait_send()

        @pl.when(cell < nc - 1)
        def _():
            neighbour_copy(k, 1).wait_send()

        pltpu.make_async_copy(pbuf.at[:, rows], pol_ref.at[:, rows], out_sem.at[k]).wait()

    @pl.when(cell < nc - 1)
    def _():
        u_copy().wait_send()


def body(n, nc, g_lesser, g_greater, w_diag, w_upper, coupled):
    size = g_lesser.shape[-1]
    shape = g_lesser.shape
    q4 = n // 4
    chunks = max(1, min(4, size // (8 * q4)))
    rows = size // q4
    block = (2, size, size)
    vmem = pl.BlockSpec(memory_space=pltpu.VMEM)
    anywhere = pl.BlockSpec(memory_space=pl.ANY)
    dma = pltpu.SemaphoreType.DMA
    out = pl.pallas_call(
        functools.partial(kernel, n, nc, chunks),
        out_shape=(jax.ShapeDtypeStruct(block, F32), jax.ShapeDtypeStruct(block, F32)),
        in_specs=[pl.BlockSpec(memory_space=pltpu.SMEM), vmem, vmem, anywhere, anywhere],
        out_specs=(anywhere, vmem),
        scratch_shapes=[
            pltpu.VMEM(block, F32),
            pltpu.VMEM((2 * q4, 2, rows, size), F32),
            pltpu.VMEM((n, 2, rows, size), F32),
            pltpu.VMEM((n, 2, rows, size), F32),
            pltpu.VMEM((3,) + block, F32),
            pltpu.VMEM(block, F32),
            pltpu.VMEM(block, F32),
            pltpu.VMEM(block, F32),
            pltpu.VMEM(block, F32),
            pltpu.VMEM(block, F32),
            pltpu.VMEM(block, F32),
            pltpu.VMEM((3, 4, 2, size, size), BF16),
            dma((chunks, q4)),
            dma((chunks, 2 * q4)),
            dma((chunks, 3, q4)),
            dma((chunks, n)),
            dma((chunks, n)),
            dma((chunks, 3, q4)),
            dma((chunks, 2)),
            dma((chunks, 2)),
            dma(()),
            dma(()),
            dma((2,)),
            dma((chunks,)),
        ],
        compiler_params=pltpu.CompilerParams(
            collective_id=0, has_side_effects=True, vmem_limit_bytes=48 * 1024 * 1024
        ),
    )(
        coupled,
        g_lesser.reshape(block),
        g_greater.reshape(block),
        w_diag.reshape(block),
        w_upper.reshape(block),
    )
    return tuple(array.reshape(shape) for array in out)


def solution(mesh):
    spec = P(None, "energy", "cell", None, None)
    return jax.shard_map(
        functools.partial(body, mesh.shape["energy"], mesh.shape["cell"]),
        mesh=mesh,
        in_specs=(spec, spec, spec, spec, P("cell")),
        out_specs=(spec, spec),
        check_vma=False,
    )
```

```python
import functools
import math

import jax
import jax.numpy as jnp
from jax import lax
from jax.experimental import pallas as pl
from jax.experimental.pallas import tpu as pltpu
from jax.sharding import PartitionSpec as P

MESH = pl.DeviceIdType.MESH
F32 = jnp.float32
BF16 = jnp.bfloat16


def split(value):
    high = value.astype(BF16)
    return high, (value - high.astype(F32)).astype(BF16)


def product(left, right):
    total = jnp.dot(left[0], right[0], preferred_element_type=F32)
    total += jnp.dot(left[0], right[1], preferred_element_type=F32)
    total += jnp.dot(left[1], right[0], preferred_element_type=F32)
    return total


def kernel(
    n, nc, chunks,
    s_ref, l_hbm, g_hbm, d_hbm, u_hbm,
    pol_ref, scr_ref,
    graw, gt, lbuf, gbuf, pout, pslab, psum, pbuf, pnext, pprev, dbuf, ubuf, uprev, parts,
    l_send, l_recv, g_send, g_recv, b_send, b_recv, lb_send, lb_recv,
    p_send, p_recv, d_send, d_recv, c_send, c_recv, u_send, u_recv, in_sem, own_sem, out_sem,
):
    me = lax.axis_index("energy")
    cell = lax.axis_index("cell")
    size = l_hbm.shape[1]
    q4 = n // 4
    quarter, j = me // q4, me % q4
    third = (quarter // 2) * (1 - quarter % 2)
    fourth = (quarter // 2) * (quarter % 2)
    span = size // chunks
    rc = span // q4

    def near(k):
        return pl.ds(k * rc, rc)

    def far(k, row_owner):
        return pl.ds(pl.multiple_of(k * span + row_owner * rc, 8), rc)

    def own_copy(k):
        return pltpu.make_async_copy(l_hbm.at[:, far(k, j)], lbuf.at[j, :, near(k)], own_sem.at[k])

    load_g = pltpu.make_async_copy(g_hbm, graw, in_sem.at[2])
    load_d = pltpu.make_async_copy(d_hbm, dbuf, in_sem.at[0])
    load_u = pltpu.make_async_copy(u_hbm, ubuf, in_sem.at[1])
    load_g.start()

    barrier = pltpu.get_barrier_semaphore()

    def greet(i, _):
        pl.semaphore_signal(barrier, inc=1, device_id=((me + i) % n, cell), device_id_type=MESH)
        return 0

    lax.fori_loop(1, n, greet, 0)

    @pl.when(cell > 0)
    def _():
        pl.semaphore_signal(barrier, inc=1, device_id=(me, cell - 1), device_id_type=MESH)

    @pl.when(cell < nc - 1)
    def _():
        pl.semaphore_signal(barrier, inc=1, device_id=(me, cell + 1), device_id_type=MESH)

    load_d.start()
    load_u.start()
    for k in range(chunks):
        own_copy(k).start()
    load_g.wait()
    for part in range(2):
        gt[part] = graw[part].T

    pl.semaphore_wait(barrier, n - 1 + jnp.minimum(cell, 1) + jnp.minimum(nc - 1 - cell, 1))

    def remote(src, dst, send, recv, energy):
        return pltpu.make_async_remote_copy(
            src_ref=src, dst_ref=dst, send_sem=send, recv_sem=recv,
            device_id=(energy, cell), device_id_type=MESH,
        )

    def l_copy(k, to):
        return remote(
            l_hbm.at[:, far(k, to)], lbuf.at[j, :, near(k)],
            l_send.at[k, to], l_recv.at[k, j], quarter * q4 + to,
        )

    def g_copy(k, to):
        return remote(
            gt.at[:, far(k, to)], gbuf.at[me, :, near(k)],
            g_send.at[k, to], g_recv.at[k, j], quarter * q4 + to,
        )

    def slab(k, step):
        ref = gbuf.at[pl.ds(quarter * q4, q4), :, near(k)]
        return remote(
            ref, ref, b_send.at[k, step + 1], b_recv.at[k, quarter], (quarter + step) * q4 + j
        )

    def l_slab(k):
        return remote(
            lbuf.at[pl.ds(0, q4), :, near(k)], lbuf.at[pl.ds(q4, q4), :, near(k)],
            lb_send.at[k], lb_recv.at[k], (quarter - 1) * q4 + j,
        )

    def p_copy(k, target):
        return remote(
            pout.at[pl.ds(target * q4, q4), :, near(k)], pslab.at[quarter, :, :, near(k)],
            p_send.at[k, target], p_recv.at[k, quarter], target * q4 + j,
        )

    def d_copy(k, to):
        return remote(
            psum.at[to, :, near(k)], pbuf.at[:, far(k, j)],
            d_send.at[k, to], d_recv.at[k, j], quarter * q4 + to,
        )

    def landed(ref, sem):
        pltpu.make_async_copy(ref, ref, sem).wait()

    for k in range(chunks):

        def spread(i, _, k=k):
            to = (j + i) % q4
            g_copy(k, to).start()
            l_copy(k, to).start()
            return 0

        lax.fori_loop(1, q4, spread, 0)

    for k in range(chunks):
        gbuf[me, :, near(k)] = gt[:, far(k, j)]

    def relay(k):
        own_copy(k).wait()

        def arrive(i, _):
            source = (j + i) % q4
            landed(gbuf.at[quarter * q4 + source, :, near(k)], g_recv.at[k, source])
            landed(lbuf.at[source, :, near(k)], l_recv.at[k, source])
            return 0

        lax.fori_loop(1, q4, arrive, 0)

        @pl.when(quarter == 0)
        def _():
            slab(k, 2).start()

        @pl.when(quarter <= 1)
        def _():
            slab(k, 1).start()

        @pl.when(quarter == 3)
        def _():
            slab(k, -1).start()
            l_slab(k).start()

    relay(0)

    load_u.wait()
    ubuf[...] = ubuf[...] * (s_ref[0].astype(F32) * 0.125)

    def u_copy():
        return pltpu.make_async_remote_copy(
            src_ref=ubuf, dst_ref=uprev, send_sem=u_send, recv_sem=u_recv,
            device_id=(me, cell + 1), device_id_type=MESH,
        )

    load_d.wait()

    def prepare(slot, ref, turn):
        for part in range(2):
            value = ref[part]
            flipped = value.T
            forward = flipped if turn else value
            backward = value if turn else flipped
            parts[slot, part, 0], parts[slot, part, 1] = split(forward)
            parts[slot, 2 + part, 0], parts[slot, 2 + part, 1] = split(backward)

    prepare(0, dbuf, False)
    if chunks > 1:
        relay(1)
    prepare(1, ubuf, False)

    @pl.when(cell < nc - 1)
    def _():
        u_copy().start()

    factor = 1.0 / math.sqrt(n)
    depth = q4 * (1 + third) * (1 - fourth)
    shifts = q4 * ((quarter + 1) * (1 - quarter // 2) + 4 * third)

    def wait_slab(k, source):
        landed(gbuf.at[pl.ds(source * q4, q4), :, near(k)], b_recv.at[k, source])

    def compute(k):
        @pl.when(quarter == 1)
        def _():
            wait_slab(k, 0)

        @pl.when(quarter == 2)
        def _():
            for source in (0, 1, 3):
                wait_slab(k, source)
            landed(lbuf.at[pl.ds(q4, q4), :, near(k)], lb_recv.at[k])

        def one_shift(w, _):
            def add(s, total):
                real, imaginary = total
                e = quarter * q4 + s - w
                lr, li = lbuf[s, 0, near(k)], lbuf[s, 1, near(k)]
                gr, gi = gbuf[e, 0, near(k)], gbuf[e, 1, near(k)]
                return real + (lr * gr - li * gi), imaginary + (lr * gi + li * gr)

            zero = jnp.zeros((rc, size), F32)
            first = jnp.maximum(w - quarter * q4, 0)
            real, imaginary = lax.fori_loop(first, depth, add, (zero, zero))
            pout[w, 0, near(k)] = imaginary * factor
            pout[w, 1, near(k)] = real * (-factor)
            return 0

        lax.fori_loop(0, shifts, one_shift, 0)

        @pl.when(quarter == 1)
        def _():
            p_copy(k, 0).start()

        @pl.when(quarter == 2)
        def _():
            for target in (0, 1, 3):
                p_copy(k, target).start()

    def combine(k):
        rows = near(k)

        @pl.when(quarter == 0)
        def _():
            landed(pslab.at[1, :, :, rows], p_recv.at[k, 1])

        @pl.when(quarter != 2)
        def _():
            landed(pslab.at[2, :, :, rows], p_recv.at[k, 2])

        def one(i, _):
            @pl.when(quarter == 0)
            def _():
                psum[i, :, rows] = pout[i, :, rows] + pslab[1, i, :, rows] + pslab[2, i, :, rows]

            @pl.when(quarter == 1)
            def _():
                psum[i, :, rows] = pout[q4 + i, :, rows] + pslab[2, i, :, rows]

            @pl.when(quarter == 2)
            def _():
                psum[i, :, rows] = pout[2 * q4 + i, :, rows]

            @pl.when(quarter == 3)
            def _():
                psum[i, :, rows] = pslab[2, i, :, rows]

            return 0

        lax.fori_loop(0, q4, one, 0)

        def spread(i, _):
            d_copy(k, (j + i) % q4).start()
            return 0

        lax.fori_loop(1, q4, spread, 0)
        pbuf[:, far(k, j)] = psum[j, :, rows]

    def neighbour_copy(k, side):
        rows = pl.ds(k * span, span)
        return pltpu.make_async_remote_copy(
            src_ref=pbuf.at[:, rows],
            dst_ref=(pnext if side == 0 else pprev).at[:, rows],
            send_sem=c_send.at[k, side],
            recv_sem=c_recv.at[k, side],
            device_id=(me, cell - 1 if side == 0 else cell + 1),
            device_id_type=MESH,
        )

    def finish(k):
        rows = pl.ds(k * span, span)

        def arrive(i, _):
            source = (j + i) % q4
            landed(pbuf.at[:, far(k, source)], d_recv.at[k, source])
            return 0

        lax.fori_loop(1, q4, arrive, 0)

        @pl.when(cell > 0)
        def _():
            neighbour_copy(k, 0).start()

        @pl.when(cell < nc - 1)
        def _():
            neighbour_copy(k, 1).start()

        pltpu.make_async_copy(pbuf.at[:, rows], pol_ref.at[:, rows], out_sem.at[k]).start()

    for k in range(chunks + 2):
        if k + 2 < chunks:
            relay(k + 2)
        if k < chunks:
            compute(k)
        if k == 0:

            @pl.when(cell > 0)
            def _():
                landed(uprev, u_recv)
                prepare(2, uprev, True)

        if 1 <= k <= chunks:
            combine(k - 1)
        if k >= 2:
            finish(k - 2)

    def term(slot, ref):
        def pair(part):
            return parts[slot, part, 0], parts[slot, part, 1]

        p_real, p_imag = split(ref[0]), split(ref[1])
        mid_real = split(product(pair(0), p_real) - product(pair(1), p_imag))
        mid_imag = split(product(pair(0), p_imag) + product(pair(1), p_real))
        real = product(mid_real, pair(2)) + product(mid_imag, pair(3))
        imaginary = product(mid_imag, pair(2)) - product(mid_real, pair(3))
        return real, imaginary

    scr_ref[0], scr_ref[1] = term(0, pbuf)

    @pl.when(cell < nc - 1)
    def _():
        for k in range(chunks):
            landed(pnext.at[:, pl.ds(k * span, span)], c_recv.at[k, 0])
        real, imaginary = term(1, pnext)
        scr_ref[0] += real
        scr_ref[1] += imaginary

    @pl.when(cell > 0)
    def _():
        for k in range(chunks):
            landed(pprev.at[:, pl.ds(k * span, span)], c_recv.at[k, 1])
        real, imaginary = term(2, pprev)
        scr_ref[0] += real
        scr_ref[1] += imaginary

    for k in range(chunks):
        rows = pl.ds(k * span, span)

        def ended(i, _, k=k):
            to = (j + i) % q4
            g_copy(k, to).wait_send()
            l_copy(k, to).wait_send()
            d_copy(k, to).wait_send()
            return 0

        lax.fori_loop(1, q4, ended, 0)

        @pl.when(quarter == 0)
        def _(k=k):
            slab(k, 2).wait_send()

        @pl.when(quarter <= 1)
        def _(k=k):
            slab(k, 1).wait_send()

        @pl.when(quarter == 3)
        def _(k=k):
            slab(k, -1).wait_send()
            l_slab(k).wait_send()

        @pl.when(quarter == 1)
        def _(k=k):
            p_copy(k, 0).wait_send()

        @pl.when(quarter == 2)
        def _(k=k):
            for target in (0, 1, 3):
                p_copy(k, target).wait_send()

        @pl.when(cell > 0)
        def _(k=k):
            neighbour_copy(k, 0).wait_send()

        @pl.when(cell < nc - 1)
        def _(k=k):
            neighbour_copy(k, 1).wait_send()

        pltpu.make_async_copy(pbuf.at[:, rows], pol_ref.at[:, rows], out_sem.at[k]).wait()

    @pl.when(cell < nc - 1)
    def _():
        u_copy().wait_send()


def body(n, nc, g_lesser, g_greater, w_diag, w_upper, coupled):
    size = g_lesser.shape[-1]
    shape = g_lesser.shape
    q4 = n // 4
    chunks = max(1, min(4, size // (8 * q4)))
    rows = size // q4
    block = (2, size, size)
    vmem = pl.BlockSpec(memory_space=pltpu.VMEM)
    anywhere = pl.BlockSpec(memory_space=pl.ANY)
    dma = pltpu.SemaphoreType.DMA
    out = pl.pallas_call(
        functools.partial(kernel, n, nc, chunks),
        out_shape=(jax.ShapeDtypeStruct(block, F32), jax.ShapeDtypeStruct(block, F32)),
        in_specs=[pl.BlockSpec(memory_space=pltpu.SMEM)] + [anywhere] * 4,
        out_specs=(anywhere, vmem),
        scratch_shapes=[
            pltpu.VMEM(block, F32),
            pltpu.VMEM(block, F32),
            pltpu.VMEM((2 * q4, 2, rows, size), F32),
            pltpu.VMEM((n, 2, rows, size), F32),
            pltpu.VMEM((n, 2, rows, size), F32),
            pltpu.VMEM((3, q4, 2, rows, size), F32),
            pltpu.VMEM((q4, 2, rows, size), F32),
            pltpu.VMEM(block, F32),
            pltpu.VMEM(block, F32),
            pltpu.VMEM(block, F32),
            pltpu.VMEM(block, F32),
            pltpu.VMEM(block, F32),
            pltpu.VMEM(block, F32),
            pltpu.VMEM((3, 4, 2, size, size), BF16),
            dma((chunks, q4)),
            dma((chunks, q4)),
            dma((chunks, q4)),
            dma((chunks, q4)),
            dma((chunks, 4)),
            dma((chunks, 4)),
            dma((chunks,)),
            dma((chunks,)),
            dma((chunks, 4)),
            dma((chunks, 3)),
            dma((chunks, q4)),
            dma((chunks, q4)),
            dma((chunks, 2)),
            dma((chunks, 2)),
            dma(()),
            dma(()),
            dma((3,)),
            dma((chunks,)),
            dma((chunks,)),
        ],
        compiler_params=pltpu.CompilerParams(
            collective_id=0, has_side_effects=True, vmem_limit_bytes=66000000
        ),
    )(
        coupled,
        g_lesser.reshape(block),
        g_greater.reshape(block),
        w_diag.reshape(block),
        w_upper.reshape(block),
    )
    return tuple(array.reshape(shape) for array in out)


def solution(mesh):
    spec = P(None, "energy", "cell", None, None)
    return jax.shard_map(
        functools.partial(body, mesh.shape["energy"], mesh.shape["cell"]),
        mesh=mesh,
        in_specs=(spec, spec, spec, spec, P("cell")),
        out_specs=(spec, spec),
        check_vma=False,
    )
```

```python
import functools
import math

import jax
import jax.numpy as jnp
from jax import lax
from jax.experimental import pallas as pl
from jax.experimental.pallas import tpu as pltpu
from jax.sharding import PartitionSpec as P

MESH = pl.DeviceIdType.MESH
F32 = jnp.float32
BF16 = jnp.bfloat16


def split(value):
    high = value.astype(BF16)
    return high, (value - high.astype(F32)).astype(BF16)


def product(left, right):
    total = jnp.dot(left[0], right[0], preferred_element_type=F32)
    total += jnp.dot(left[0], right[1], preferred_element_type=F32)
    total += jnp.dot(left[1], right[0], preferred_element_type=F32)
    return total


def kernel(
    n, nc, chunks,
    s_ref, l_hbm, g_hbm, d_hbm, u_hbm,
    pol_ref, scr_ref,
    graw, gt, lbuf, gbuf, pout, pslab, psum, pbuf, pnext, pprev, dbuf, ubuf, uprev, parts, mid,
    l_send, l_recv, g_send, g_recv, b_send, b_recv, lb_send, lb_recv,
    p_send, p_recv, d_send, d_recv, c_send, c_recv, u_send, u_recv, in_sem, own_sem, out_sem,
):
    me = lax.axis_index("energy")
    cell = lax.axis_index("cell")
    size = l_hbm.shape[1]
    q4 = n // 4
    quarter, j = me // q4, me % q4
    third = (quarter // 2) * (1 - quarter % 2)
    fourth = (quarter // 2) * (quarter % 2)
    span = size // chunks
    rc = span // q4

    def near(k):
        return pl.ds(k * rc, rc)

    def far(k, row_owner):
        return pl.ds(pl.multiple_of(k * span + row_owner * rc, 8), rc)

    def own_copy(k):
        return pltpu.make_async_copy(l_hbm.at[:, far(k, j)], lbuf.at[j, :, near(k)], own_sem.at[k])

    load_g = pltpu.make_async_copy(g_hbm, graw, in_sem.at[2])
    load_d = pltpu.make_async_copy(d_hbm, dbuf, in_sem.at[0])
    load_u = pltpu.make_async_copy(u_hbm, ubuf, in_sem.at[1])
    load_g.start()

    barrier = pltpu.get_barrier_semaphore()

    def greet(i, _):
        pl.semaphore_signal(barrier, inc=1, device_id=((me + i) % n, cell), device_id_type=MESH)
        return 0

    lax.fori_loop(1, n, greet, 0)

    @pl.when(cell > 0)
    def _():
        pl.semaphore_signal(barrier, inc=1, device_id=(me, cell - 1), device_id_type=MESH)

    @pl.when(cell < nc - 1)
    def _():
        pl.semaphore_signal(barrier, inc=1, device_id=(me, cell + 1), device_id_type=MESH)

    load_d.start()
    load_u.start()
    for k in range(chunks):
        own_copy(k).start()
    load_g.wait()
    for part in range(2):
        gt[part] = graw[part].T

    pl.semaphore_wait(barrier, n - 1 + jnp.minimum(cell, 1) + jnp.minimum(nc - 1 - cell, 1))

    def remote(src, dst, send, recv, energy):
        return pltpu.make_async_remote_copy(
            src_ref=src, dst_ref=dst, send_sem=send, recv_sem=recv,
            device_id=(energy, cell), device_id_type=MESH,
        )

    def l_copy(k, to):
        return remote(
            l_hbm.at[:, far(k, to)], lbuf.at[j, :, near(k)],
            l_send.at[k, to], l_recv.at[k, j], quarter * q4 + to,
        )

    def g_copy(k, to):
        return remote(
            gt.at[:, far(k, to)], gbuf.at[me, :, near(k)],
            g_send.at[k, to], g_recv.at[k, j], quarter * q4 + to,
        )

    def slab(k, step):
        ref = gbuf.at[pl.ds(quarter * q4, q4), :, near(k)]
        return remote(
            ref, ref, b_send.at[k, step + 1], b_recv.at[k, quarter], (quarter + step) * q4 + j
        )

    def l_slab(k):
        return remote(
            lbuf.at[pl.ds(0, q4), :, near(k)], lbuf.at[pl.ds(q4, q4), :, near(k)],
            lb_send.at[k], lb_recv.at[k], (quarter - 1) * q4 + j,
        )

    def p_copy(k, target):
        return remote(
            pout.at[pl.ds(target * q4, q4), :, near(k)], pslab.at[quarter, :, :, near(k)],
            p_send.at[k, target], p_recv.at[k, quarter], target * q4 + j,
        )

    def d_copy(k, to):
        return remote(
            psum.at[to, :, near(k)], pbuf.at[:, far(k, j)],
            d_send.at[k, to], d_recv.at[k, j], quarter * q4 + to,
        )

    def landed(ref, sem):
        pltpu.make_async_copy(ref, ref, sem).wait()

    for k in range(chunks):

        def spread(i, _, k=k):
            to = (j + i) % q4
            g_copy(k, to).start()
            l_copy(k, to).start()
            return 0

        lax.fori_loop(1, q4, spread, 0)

    for k in range(chunks):
        gbuf[me, :, near(k)] = gt[:, far(k, j)]

    def relay(k):
        own_copy(k).wait()

        def arrive(i, _):
            source = (j + i) % q4
            landed(gbuf.at[quarter * q4 + source, :, near(k)], g_recv.at[k, source])
            landed(lbuf.at[source, :, near(k)], l_recv.at[k, source])
            return 0

        lax.fori_loop(1, q4, arrive, 0)

        @pl.when(quarter == 0)
        def _():
            slab(k, 2).start()

        @pl.when(quarter <= 1)
        def _():
            slab(k, 1).start()

        @pl.when(quarter == 3)
        def _():
            slab(k, -1).start()
            l_slab(k).start()

    relay(0)

    load_u.wait()
    ubuf[...] = ubuf[...] * (s_ref[0].astype(F32) * 0.125)

    def u_copy():
        return pltpu.make_async_remote_copy(
            src_ref=ubuf, dst_ref=uprev, send_sem=u_send, recv_sem=u_recv,
            device_id=(me, cell + 1), device_id_type=MESH,
        )

    load_d.wait()

    def prepare(slot, ref, turn):
        for part in range(2):
            value = ref[part]
            flipped = value.T
            forward = flipped if turn else value
            backward = value if turn else flipped
            parts[slot, part, 0], parts[slot, part, 1] = split(forward)
            parts[slot, 2 + part, 0], parts[slot, 2 + part, 1] = split(backward)

    prepare(0, dbuf, False)
    if chunks > 1:
        relay(1)
    prepare(1, ubuf, False)

    @pl.when(cell < nc - 1)
    def _():
        u_copy().start()

    factor = 1.0 / math.sqrt(n)
    depth = q4 * (1 + third) * (1 - fourth)
    shifts = q4 * ((quarter + 1) * (1 - quarter // 2) + 4 * third)

    def wait_slab(k, source):
        landed(gbuf.at[pl.ds(source * q4, q4), :, near(k)], b_recv.at[k, source])

    def compute(k):
        @pl.when(quarter == 1)
        def _():
            wait_slab(k, 0)

        @pl.when(quarter == 2)
        def _():
            for source in (0, 1, 3):
                wait_slab(k, source)
            landed(lbuf.at[pl.ds(q4, q4), :, near(k)], lb_recv.at[k])

        def one_shift(w, _):
            def add(s, total):
                real, imaginary = total
                e = quarter * q4 + s - w
                lr, li = lbuf[s, 0, near(k)], lbuf[s, 1, near(k)]
                gr, gi = gbuf[e, 0, near(k)], gbuf[e, 1, near(k)]
                return real + (lr * gr - li * gi), imaginary + (lr * gi + li * gr)

            zero = jnp.zeros((rc, size), F32)
            first = jnp.maximum(w - quarter * q4, 0)
            real, imaginary = lax.fori_loop(first, depth, add, (zero, zero))
            pout[w, 0, near(k)] = imaginary * factor
            pout[w, 1, near(k)] = real * (-factor)
            return 0

        lax.fori_loop(0, shifts, one_shift, 0)

        @pl.when(quarter == 1)
        def _():
            p_copy(k, 0).start()

        @pl.when(quarter == 2)
        def _():
            for target in (0, 1, 3):
                p_copy(k, target).start()

    def combine(k):
        rows = near(k)

        @pl.when(quarter == 0)
        def _():
            landed(pslab.at[1, :, :, rows], p_recv.at[k, 1])

        @pl.when(quarter != 2)
        def _():
            landed(pslab.at[2, :, :, rows], p_recv.at[k, 2])

        def one(i, _):
            @pl.when(quarter == 0)
            def _():
                psum[i, :, rows] = pout[i, :, rows] + pslab[1, i, :, rows] + pslab[2, i, :, rows]

            @pl.when(quarter == 1)
            def _():
                psum[i, :, rows] = pout[q4 + i, :, rows] + pslab[2, i, :, rows]

            @pl.when(quarter == 2)
            def _():
                psum[i, :, rows] = pout[2 * q4 + i, :, rows]

            @pl.when(quarter == 3)
            def _():
                psum[i, :, rows] = pslab[2, i, :, rows]

            return 0

        lax.fori_loop(0, q4, one, 0)

        def spread(i, _):
            d_copy(k, (j + i) % q4).start()
            return 0

        lax.fori_loop(1, q4, spread, 0)
        pbuf[:, far(k, j)] = psum[j, :, rows]

    def neighbour_copy(k, side):
        rows = pl.ds(k * span, span)
        return pltpu.make_async_remote_copy(
            src_ref=pbuf.at[:, rows],
            dst_ref=(pnext if side == 0 else pprev).at[:, rows],
            send_sem=c_send.at[k, side],
            recv_sem=c_recv.at[k, side],
            device_id=(me, cell - 1 if side == 0 else cell + 1),
            device_id_type=MESH,
        )

    def finish(k):
        rows = pl.ds(k * span, span)

        def arrive(i, _):
            source = (j + i) % q4
            landed(pbuf.at[:, far(k, source)], d_recv.at[k, source])
            return 0

        lax.fori_loop(1, q4, arrive, 0)

        @pl.when(cell > 0)
        def _():
            neighbour_copy(k, 0).start()

        @pl.when(cell < nc - 1)
        def _():
            neighbour_copy(k, 1).start()

        pltpu.make_async_copy(pbuf.at[:, rows], pol_ref.at[:, rows], out_sem.at[k]).start()

    def pair(slot, part):
        return parts[slot, part, 0], parts[slot, part, 1]

    def right_product(slot, ref, first, last):
        rows = pl.ds(first * span, (last - first) * span)
        p_real, p_imag = split(ref[0, rows]), split(ref[1, rows])
        real = product(p_real, pair(slot, 2)) + product(p_imag, pair(slot, 3))
        imaginary = product(p_imag, pair(slot, 2)) - product(p_real, pair(slot, 3))
        mid[slot, 0, 0, rows], mid[slot, 0, 1, rows] = split(real)
        mid[slot, 1, 0, rows], mid[slot, 1, 1, rows] = split(imaginary)

    def left_product(slot):
        m_real, m_imag = (mid[slot, 0, 0], mid[slot, 0, 1]), (mid[slot, 1, 0], mid[slot, 1, 1])
        real = product(pair(slot, 0), m_real) - product(pair(slot, 1), m_imag)
        imaginary = product(pair(slot, 0), m_imag) + product(pair(slot, 1), m_real)
        return real, imaginary

    def from_neighbour(side, first, last, whole):
        @pl.when(cell < nc - 1 if side == 0 else cell > 0)
        def _():
            ref = pnext if side == 0 else pprev
            for k in range(first, last):
                landed(ref.at[:, pl.ds(k * span, span)], c_recv.at[k, side])
            right_product(side + 1, ref, first, last)
            if whole:
                real, imaginary = left_product(side + 1)
                scr_ref[0] += real
                scr_ref[1] += imaginary

    bounds = sorted({0, chunks // 2, chunks - 1, chunks})
    batches = list(zip(bounds[:-1], bounds[1:]))
    for k in range(chunks + 2):
        if k + 2 < chunks:
            relay(k + 2)
        if k < chunks:
            compute(k)
        if k == 0:

            @pl.when(cell > 0)
            def _():
                landed(uprev, u_recv)
                prepare(2, uprev, True)

        if 1 <= k <= chunks:
            combine(k - 1)
        if k >= 2:
            finish(k - 2)
        for first, last in batches[:-1]:
            if k == last + 1:
                right_product(0, pbuf, first, last)
            if k == last + 2:
                from_neighbour(0, first, last, False)
                from_neighbour(1, first, last, False)

    right_product(0, pbuf, *batches[-1])
    scr_ref[0], scr_ref[1] = left_product(0)

    @pl.when(cell % 2 == 0)
    def _():
        from_neighbour(0, *batches[-1], True)
        from_neighbour(1, *batches[-1], True)

    @pl.when(cell % 2 == 1)
    def _():
        from_neighbour(1, *batches[-1], True)
        from_neighbour(0, *batches[-1], True)

    for k in range(chunks):
        rows = pl.ds(k * span, span)

        def ended(i, _, k=k):
            to = (j + i) % q4
            g_copy(k, to).wait_send()
            l_copy(k, to).wait_send()
            d_copy(k, to).wait_send()
            return 0

        lax.fori_loop(1, q4, ended, 0)

        @pl.when(quarter == 0)
        def _(k=k):
            slab(k, 2).wait_send()

        @pl.when(quarter <= 1)
        def _(k=k):
            slab(k, 1).wait_send()

        @pl.when(quarter == 3)
        def _(k=k):
            slab(k, -1).wait_send()
            l_slab(k).wait_send()

        @pl.when(quarter == 1)
        def _(k=k):
            p_copy(k, 0).wait_send()

        @pl.when(quarter == 2)
        def _(k=k):
            for target in (0, 1, 3):
                p_copy(k, target).wait_send()

        @pl.when(cell > 0)
        def _(k=k):
            neighbour_copy(k, 0).wait_send()

        @pl.when(cell < nc - 1)
        def _(k=k):
            neighbour_copy(k, 1).wait_send()

        pltpu.make_async_copy(pbuf.at[:, rows], pol_ref.at[:, rows], out_sem.at[k]).wait()

    @pl.when(cell < nc - 1)
    def _():
        u_copy().wait_send()


def body(n, nc, g_lesser, g_greater, w_diag, w_upper, coupled):
    size = g_lesser.shape[-1]
    shape = g_lesser.shape
    q4 = n // 4
    chunks = max(1, min(8, size // (8 * q4)))
    rows = size // q4
    block = (2, size, size)
    vmem = pl.BlockSpec(memory_space=pltpu.VMEM)
    anywhere = pl.BlockSpec(memory_space=pl.ANY)
    dma = pltpu.SemaphoreType.DMA
    out = pl.pallas_call(
        functools.partial(kernel, n, nc, chunks),
        out_shape=(jax.ShapeDtypeStruct(block, F32), jax.ShapeDtypeStruct(block, F32)),
        in_specs=[pl.BlockSpec(memory_space=pltpu.SMEM)] + [anywhere] * 4,
        out_specs=(anywhere, vmem),
        scratch_shapes=[
            pltpu.VMEM(block, F32),
            pltpu.VMEM(block, F32),
            pltpu.VMEM((2 * q4, 2, rows, size), F32),
            pltpu.VMEM((n, 2, rows, size), F32),
            pltpu.VMEM((n, 2, rows, size), F32),
            pltpu.VMEM((3, q4, 2, rows, size), F32),
            pltpu.VMEM((q4, 2, rows, size), F32),
            pltpu.VMEM(block, F32),
            pltpu.VMEM(block, F32),
            pltpu.VMEM(block, F32),
            pltpu.VMEM(block, F32),
            pltpu.VMEM(block, F32),
            pltpu.VMEM(block, F32),
            pltpu.VMEM((3, 4, 2, size, size), BF16),
            pltpu.VMEM((3, 2, 2, size, size), BF16),
            dma((chunks, q4)),
            dma((chunks, q4)),
            dma((chunks, q4)),
            dma((chunks, q4)),
            dma((chunks, 4)),
            dma((chunks, 4)),
            dma((chunks,)),
            dma((chunks,)),
            dma((chunks, 4)),
            dma((chunks, 3)),
            dma((chunks, q4)),
            dma((chunks, q4)),
            dma((chunks, 2)),
            dma((chunks, 2)),
            dma(()),
            dma(()),
            dma((3,)),
            dma((chunks,)),
            dma((chunks,)),
        ],
        compiler_params=pltpu.CompilerParams(
            collective_id=0, has_side_effects=True, vmem_limit_bytes=66000000
        ),
    )(
        coupled,
        g_lesser.reshape(block),
        g_greater.reshape(block),
        w_diag.reshape(block),
        w_upper.reshape(block),
    )
    return tuple(array.reshape(shape) for array in out)


def solution(mesh):
    spec = P(None, "energy", "cell", None, None)
    return jax.shard_map(
        functools.partial(body, mesh.shape["energy"], mesh.shape["cell"]),
        mesh=mesh,
        in_specs=(spec, spec, spec, spec, P("cell")),
        out_specs=(spec, spec),
        check_vma=False,
    )
```

```python
import functools
import math

import jax
import jax.numpy as jnp
from jax import lax
from jax.experimental import pallas as pl
from jax.experimental.pallas import tpu as pltpu
from jax.sharding import PartitionSpec as P

MESH = pl.DeviceIdType.MESH
F32 = jnp.float32
BF16 = jnp.bfloat16


def split(value):
    high = value.astype(BF16)
    return high, (value - high.astype(F32)).astype(BF16)


def product(left, right):
    total = jnp.dot(left[0], right[0], preferred_element_type=F32)
    total += jnp.dot(left[0], right[1], preferred_element_type=F32)
    total += jnp.dot(left[1], right[0], preferred_element_type=F32)
    return total


def kernel(
    n, nc, chunks,
    s_ref, l_hbm, g_hbm, d_hbm, u_hbm,
    pol_ref, scr_ref,
    graw, gt, lbuf, gbuf, pout, pslab, psum, pbuf, pnext, pprev, dbuf, ubuf, uprev, parts, mid,
    l_send, l_recv, g_send, g_recv, b_send, b_recv, lb_send, lb_recv,
    p_send, p_recv, d_send, d_recv, c_send, c_recv, u_send, u_recv, in_sem, own_sem, out_sem,
):
    me = lax.axis_index("energy")
    cell = lax.axis_index("cell")
    size = l_hbm.shape[1]
    q4 = n // 4
    quarter, j = me // q4, me % q4
    third = (quarter // 2) * (1 - quarter % 2)
    fourth = (quarter // 2) * (quarter % 2)
    span = size // chunks
    rc = span // q4

    def near(k):
        return pl.ds(k * rc, rc)

    def far(k, row_owner):
        return pl.ds(pl.multiple_of(k * span + row_owner * rc, 8), rc)

    def own_copy(k):
        return pltpu.make_async_copy(l_hbm.at[:, far(k, j)], lbuf.at[j, :, near(k)], own_sem.at[k])

    load_g = pltpu.make_async_copy(g_hbm, graw, in_sem.at[2])
    load_d = pltpu.make_async_copy(d_hbm, dbuf, in_sem.at[0])
    load_u = pltpu.make_async_copy(u_hbm, ubuf, in_sem.at[1])
    load_g.start()

    barrier = pltpu.get_barrier_semaphore()

    def greet(i, _):
        pl.semaphore_signal(barrier, inc=1, device_id=((me + i) % n, cell), device_id_type=MESH)
        return 0

    lax.fori_loop(1, n, greet, 0)

    @pl.when(cell > 0)
    def _():
        pl.semaphore_signal(barrier, inc=1, device_id=(me, cell - 1), device_id_type=MESH)

    @pl.when(cell < nc - 1)
    def _():
        pl.semaphore_signal(barrier, inc=1, device_id=(me, cell + 1), device_id_type=MESH)

    load_d.start()
    load_u.start()
    for k in range(chunks):
        own_copy(k).start()
    load_g.wait()
    for part in range(2):
        gt[part] = graw[part].T

    pl.semaphore_wait(barrier, n - 1 + jnp.minimum(cell, 1) + jnp.minimum(nc - 1 - cell, 1))

    def remote(src, dst, send, recv, energy):
        return pltpu.make_async_remote_copy(
            src_ref=src, dst_ref=dst, send_sem=send, recv_sem=recv,
            device_id=(energy, cell), device_id_type=MESH,
        )

    def l_copy(k, to):
        return remote(
            l_hbm.at[:, far(k, to)], lbuf.at[j, :, near(k)],
            l_send.at[k, to], l_recv.at[k, j], quarter * q4 + to,
        )

    def g_copy(k, to):
        return remote(
            gt.at[:, far(k, to)], gbuf.at[me, :, near(k)],
            g_send.at[k, to], g_recv.at[k, j], quarter * q4 + to,
        )

    def slab(k, step):
        ref = gbuf.at[pl.ds(quarter * q4, q4), :, near(k)]
        return remote(
            ref, ref, b_send.at[k, step + 1], b_recv.at[k, quarter], (quarter + step) * q4 + j
        )

    def l_slab(k):
        return remote(
            lbuf.at[pl.ds(0, q4), :, near(k)], lbuf.at[pl.ds(q4, q4), :, near(k)],
            lb_send.at[k], lb_recv.at[k], (quarter - 1) * q4 + j,
        )

    def p_copy(k, target):
        return remote(
            pout.at[pl.ds(target * q4, q4), :, near(k)], pslab.at[quarter, :, :, near(k)],
            p_send.at[k, target], p_recv.at[k, quarter], target * q4 + j,
        )

    def d_copy(k, to):
        return remote(
            psum.at[to, :, near(k)], pbuf.at[:, far(k, j)],
            d_send.at[k, to], d_recv.at[k, j], quarter * q4 + to,
        )

    def landed(ref, sem):
        pltpu.make_async_copy(ref, ref, sem).wait()

    for k in range(chunks):

        def spread(i, _, k=k):
            to = (j + i) % q4
            g_copy(k, to).start()
            l_copy(k, to).start()
            return 0

        lax.fori_loop(1, q4, spread, 0)

    load_u.wait()
    ubuf[...] = ubuf[...] * (s_ref[0].astype(F32) * 0.125)

    def u_copy():
        return pltpu.make_async_remote_copy(
            src_ref=ubuf, dst_ref=uprev, send_sem=u_send, recv_sem=u_recv,
            device_id=(me, cell + 1), device_id_type=MESH,
        )

    for k in range(chunks):
        gbuf[me, :, near(k)] = gt[:, far(k, j)]

    @pl.when(cell < nc - 1)
    def _():
        u_copy().start()

    def relay(k):
        own_copy(k).wait()

        def arrive(i, _):
            source = (j + i) % q4
            landed(gbuf.at[quarter * q4 + source, :, near(k)], g_recv.at[k, source])
            landed(lbuf.at[source, :, near(k)], l_recv.at[k, source])
            return 0

        lax.fori_loop(1, q4, arrive, 0)

        @pl.when(quarter == 0)
        def _():
            slab(k, 2).start()

        @pl.when(quarter <= 1)
        def _():
            slab(k, 1).start()

        @pl.when(quarter == 3)
        def _():
            slab(k, -1).start()
            l_slab(k).start()

    relay(0)

    load_d.wait()

    def prepare(slot, ref, turn):
        for part in range(2):
            value = ref[part]
            flipped = value.T
            forward = flipped if turn else value
            backward = value if turn else flipped
            parts[slot, part, 0], parts[slot, part, 1] = split(forward)
            parts[slot, 2 + part, 0], parts[slot, 2 + part, 1] = split(backward)

    prepare(0, dbuf, False)
    ahead = min(4, chunks)
    if ahead > 1:
        relay(1)
    prepare(1, ubuf, False)
    for k in range(2, ahead):
        relay(k)

    factor = 1.0 / math.sqrt(n)
    depth = q4 * (1 + third) * (1 - fourth)
    shifts = q4 * ((quarter + 1) * (1 - quarter // 2) + 4 * third)

    def wait_slab(k, source):
        landed(gbuf.at[pl.ds(source * q4, q4), :, near(k)], b_recv.at[k, source])

    def compute(k):
        @pl.when(quarter == 1)
        def _():
            wait_slab(k, 0)

        @pl.when(quarter == 2)
        def _():
            for source in (0, 1, 3):
                wait_slab(k, source)
            landed(lbuf.at[pl.ds(q4, q4), :, near(k)], lb_recv.at[k])

        def one_shift(w, _):
            def add(s, total):
                real, imaginary = total
                e = quarter * q4 + s - w
                lr, li = lbuf[s, 0, near(k)], lbuf[s, 1, near(k)]
                gr, gi = gbuf[e, 0, near(k)], gbuf[e, 1, near(k)]
                return real + (lr * gr - li * gi), imaginary + (lr * gi + li * gr)

            zero = jnp.zeros((rc, size), F32)
            first = jnp.maximum(w - quarter * q4, 0)
            real, imaginary = lax.fori_loop(first, depth, add, (zero, zero))
            pout[w, 0, near(k)] = imaginary * factor
            pout[w, 1, near(k)] = real * (-factor)
            return 0

        lax.fori_loop(0, shifts, one_shift, 0)

        @pl.when(quarter == 1)
        def _():
            p_copy(k, 0).start()

        @pl.when(quarter == 2)
        def _():
            for target in (0, 1, 3):
                p_copy(k, target).start()

    def combine(k):
        rows = near(k)

        @pl.when(quarter == 0)
        def _():
            landed(pslab.at[1, :, :, rows], p_recv.at[k, 1])

        @pl.when(quarter != 2)
        def _():
            landed(pslab.at[2, :, :, rows], p_recv.at[k, 2])

        def one(i, _):
            @pl.when(quarter == 0)
            def _():
                psum[i, :, rows] = pout[i, :, rows] + pslab[1, i, :, rows] + pslab[2, i, :, rows]

            @pl.when(quarter == 1)
            def _():
                psum[i, :, rows] = pout[q4 + i, :, rows] + pslab[2, i, :, rows]

            @pl.when(quarter == 2)
            def _():
                psum[i, :, rows] = pout[2 * q4 + i, :, rows]

            @pl.when(quarter == 3)
            def _():
                psum[i, :, rows] = pslab[2, i, :, rows]

            return 0

        lax.fori_loop(0, q4, one, 0)

        def spread(i, _):
            d_copy(k, (j + i) % q4).start()
            return 0

        lax.fori_loop(1, q4, spread, 0)
        pbuf[:, far(k, j)] = psum[j, :, rows]

    def neighbour_copy(k, side):
        rows = pl.ds(k * span, span)
        return pltpu.make_async_remote_copy(
            src_ref=pbuf.at[:, rows],
            dst_ref=(pnext if side == 0 else pprev).at[:, rows],
            send_sem=c_send.at[k, side],
            recv_sem=c_recv.at[k, side],
            device_id=(me, cell - 1 if side == 0 else cell + 1),
            device_id_type=MESH,
        )

    def finish(k):
        rows = pl.ds(k * span, span)

        def arrive(i, _):
            source = (j + i) % q4
            landed(pbuf.at[:, far(k, source)], d_recv.at[k, source])
            return 0

        lax.fori_loop(1, q4, arrive, 0)

        @pl.when(cell > 0)
        def _():
            neighbour_copy(k, 0).start()

        @pl.when(cell < nc - 1)
        def _():
            neighbour_copy(k, 1).start()

        pltpu.make_async_copy(pbuf.at[:, rows], pol_ref.at[:, rows], out_sem.at[k]).start()

    def pair(slot, part):
        return parts[slot, part, 0], parts[slot, part, 1]

    def right_product(slot, ref, first, last):
        rows = pl.ds(first * span, (last - first) * span)
        p_real, p_imag = split(ref[0, rows]), split(ref[1, rows])
        real = product(p_real, pair(slot, 2)) + product(p_imag, pair(slot, 3))
        imaginary = product(p_imag, pair(slot, 2)) - product(p_real, pair(slot, 3))
        mid[slot, 0, 0, rows], mid[slot, 0, 1, rows] = split(real)
        mid[slot, 1, 0, rows], mid[slot, 1, 1, rows] = split(imaginary)

    def left_product(slot):
        m_real, m_imag = (mid[slot, 0, 0], mid[slot, 0, 1]), (mid[slot, 1, 0], mid[slot, 1, 1])
        real = product(pair(slot, 0), m_real) - product(pair(slot, 1), m_imag)
        imaginary = product(pair(slot, 0), m_imag) + product(pair(slot, 1), m_real)
        return real, imaginary

    def from_neighbour(side, first, last, whole):
        @pl.when(cell < nc - 1 if side == 0 else cell > 0)
        def _():
            ref = pnext if side == 0 else pprev
            for k in range(first, last):
                landed(ref.at[:, pl.ds(k * span, span)], c_recv.at[k, side])
            right_product(side + 1, ref, first, last)
            if whole:
                real, imaginary = left_product(side + 1)
                scr_ref[0] += real
                scr_ref[1] += imaginary

    bounds = sorted({0, chunks // 2, chunks - 1, chunks})
    batches = list(zip(bounds[:-1], bounds[1:]))
    for k in range(chunks + 2):
        if k + ahead < chunks:
            relay(k + ahead)
        if k < chunks:
            compute(k)
        if k == chunks // 4:

            @pl.when(cell > 0)
            def _():
                landed(uprev, u_recv)
                prepare(2, uprev, True)

        if 1 <= k <= chunks:
            combine(k - 1)
        if k >= 2:
            finish(k - 2)
        for first, last in batches[:-1]:
            if k == last + 1:
                right_product(0, pbuf, first, last)
            if k == last + 2:
                from_neighbour(0, first, last, False)
                from_neighbour(1, first, last, False)

    right_product(0, pbuf, *batches[-1])
    scr_ref[0], scr_ref[1] = left_product(0)

    @pl.when(cell % 2 == 0)
    def _():
        from_neighbour(0, *batches[-1], True)
        from_neighbour(1, *batches[-1], True)

    @pl.when(cell % 2 == 1)
    def _():
        from_neighbour(1, *batches[-1], True)
        from_neighbour(0, *batches[-1], True)

    for k in range(chunks):
        rows = pl.ds(k * span, span)

        def ended(i, _, k=k):
            to = (j + i) % q4
            g_copy(k, to).wait_send()
            l_copy(k, to).wait_send()
            d_copy(k, to).wait_send()
            return 0

        lax.fori_loop(1, q4, ended, 0)

        @pl.when(quarter == 0)
        def _(k=k):
            slab(k, 2).wait_send()

        @pl.when(quarter <= 1)
        def _(k=k):
            slab(k, 1).wait_send()

        @pl.when(quarter == 3)
        def _(k=k):
            slab(k, -1).wait_send()
            l_slab(k).wait_send()

        @pl.when(quarter == 1)
        def _(k=k):
            p_copy(k, 0).wait_send()

        @pl.when(quarter == 2)
        def _(k=k):
            for target in (0, 1, 3):
                p_copy(k, target).wait_send()

        @pl.when(cell > 0)
        def _(k=k):
            neighbour_copy(k, 0).wait_send()

        @pl.when(cell < nc - 1)
        def _(k=k):
            neighbour_copy(k, 1).wait_send()

        pltpu.make_async_copy(pbuf.at[:, rows], pol_ref.at[:, rows], out_sem.at[k]).wait()

    @pl.when(cell < nc - 1)
    def _():
        u_copy().wait_send()


def body(n, nc, g_lesser, g_greater, w_diag, w_upper, coupled):
    size = g_lesser.shape[-1]
    shape = g_lesser.shape
    q4 = n // 4
    chunks = max(1, min(8, size // (8 * q4)))
    rows = size // q4
    block = (2, size, size)
    vmem = pl.BlockSpec(memory_space=pltpu.VMEM)
    anywhere = pl.BlockSpec(memory_space=pl.ANY)
    dma = pltpu.SemaphoreType.DMA
    out = pl.pallas_call(
        functools.partial(kernel, n, nc, chunks),
        out_shape=(jax.ShapeDtypeStruct(block, F32), jax.ShapeDtypeStruct(block, F32)),
        in_specs=[pl.BlockSpec(memory_space=pltpu.SMEM)] + [anywhere] * 4,
        out_specs=(anywhere, vmem),
        scratch_shapes=[
            pltpu.VMEM(block, F32),
            pltpu.VMEM(block, F32),
            pltpu.VMEM((2 * q4, 2, rows, size), F32),
            pltpu.VMEM((n, 2, rows, size), F32),
            pltpu.VMEM((n, 2, rows, size), F32),
            pltpu.VMEM((3, q4, 2, rows, size), F32),
            pltpu.VMEM((q4, 2, rows, size), F32),
            pltpu.VMEM(block, F32),
            pltpu.VMEM(block, F32),
            pltpu.VMEM(block, F32),
            pltpu.VMEM(block, F32),
            pltpu.VMEM(block, F32),
            pltpu.VMEM(block, F32),
            pltpu.VMEM((3, 4, 2, size, size), BF16),
            pltpu.VMEM((3, 2, 2, size, size), BF16),
            dma((chunks, q4)),
            dma((chunks, q4)),
            dma((chunks, q4)),
            dma((chunks, q4)),
            dma((chunks, 4)),
            dma((chunks, 4)),
            dma((chunks,)),
            dma((chunks,)),
            dma((chunks, 4)),
            dma((chunks, 3)),
            dma((chunks, q4)),
            dma((chunks, q4)),
            dma((chunks, 2)),
            dma((chunks, 2)),
            dma(()),
            dma(()),
            dma((3,)),
            dma((chunks,)),
            dma((chunks,)),
        ],
        compiler_params=pltpu.CompilerParams(
            collective_id=0, has_side_effects=True, vmem_limit_bytes=66000000
        ),
    )(
        coupled,
        g_lesser.reshape(block),
        g_greater.reshape(block),
        w_diag.reshape(block),
        w_upper.reshape(block),
    )
    return tuple(array.reshape(shape) for array in out)


def solution(mesh):
    spec = P(None, "energy", "cell", None, None)
    return jax.shard_map(
        functools.partial(body, mesh.shape["energy"], mesh.shape["cell"]),
        mesh=mesh,
        in_specs=(spec, spec, spec, spec, P("cell")),
        out_specs=(spec, spec),
        check_vma=False,
    )
```

```python
import functools
import math

import jax
import jax.numpy as jnp
from jax import lax
from jax.experimental import pallas as pl
from jax.experimental.pallas import tpu as pltpu
from jax.sharding import PartitionSpec as P

MESH = pl.DeviceIdType.MESH
F32 = jnp.float32
BF16 = jnp.bfloat16


def split(value):
    high = value.astype(BF16)
    return high, (value - high.astype(F32)).astype(BF16)


def product(left, right):
    total = jnp.dot(left[0], right[0], preferred_element_type=F32)
    total += jnp.dot(left[0], right[1], preferred_element_type=F32)
    total += jnp.dot(left[1], right[0], preferred_element_type=F32)
    return total


def kernel(
    n, nc, chunks,
    s_ref, l_hbm, g_hbm, d_hbm, u_hbm,
    pol_ref, scr_ref,
    graw, gt, lbuf, gbuf, pout, pslab, psum, pbuf, pnext, pprev, dbuf, ubuf, uprev, parts, mid,
    l_send, l_recv, g_send, g_recv, b_send, b_recv, lb_send, lb_recv,
    p_send, p_recv, d_send, d_recv, c_send, c_recv, u_send, u_recv, in_sem, own_sem, out_sem,
):
    me = lax.axis_index("energy")
    cell = lax.axis_index("cell")
    size = l_hbm.shape[1]
    q4 = n // 4
    quarter, j = me // q4, me % q4
    third = (quarter // 2) * (1 - quarter % 2)
    fourth = (quarter // 2) * (quarter % 2)
    span = size // chunks
    rc = span // q4

    def near(k):
        return pl.ds(k * rc, rc)

    def far(k, row_owner):
        return pl.ds(pl.multiple_of(k * span + row_owner * rc, 8), rc)

    def own_copy(k):
        return pltpu.make_async_copy(l_hbm.at[:, far(k, j)], lbuf.at[j, :, near(k)], own_sem.at[k])

    load_g = pltpu.make_async_copy(g_hbm, graw, in_sem.at[2])
    load_d = pltpu.make_async_copy(d_hbm, dbuf, in_sem.at[0])
    load_u = pltpu.make_async_copy(u_hbm, ubuf, in_sem.at[1])
    load_g.start()

    barrier = pltpu.get_barrier_semaphore()

    def greet(i, _):
        pl.semaphore_signal(barrier, inc=1, device_id=((me + i) % n, cell), device_id_type=MESH)
        return 0

    lax.fori_loop(1, n, greet, 0)

    @pl.when(cell > 0)
    def _():
        pl.semaphore_signal(barrier, inc=1, device_id=(me, cell - 1), device_id_type=MESH)

    @pl.when(cell < nc - 1)
    def _():
        pl.semaphore_signal(barrier, inc=1, device_id=(me, cell + 1), device_id_type=MESH)

    load_d.start()
    load_u.start()
    for k in range(chunks):
        own_copy(k).start()
    load_g.wait()
    for part in range(2):
        gt[part] = graw[part].T

    pl.semaphore_wait(barrier, n - 1 + jnp.minimum(cell, 1) + jnp.minimum(nc - 1 - cell, 1))

    def remote(src, dst, send, recv, energy):
        return pltpu.make_async_remote_copy(
            src_ref=src, dst_ref=dst, send_sem=send, recv_sem=recv,
            device_id=(energy, cell), device_id_type=MESH,
        )

    def l_copy(k, to):
        return remote(
            l_hbm.at[:, far(k, to)], lbuf.at[j, :, near(k)],
            l_send.at[k, to], l_recv.at[k, j], quarter * q4 + to,
        )

    def g_copy(k, to):
        return remote(
            gt.at[:, far(k, to)], gbuf.at[me, :, near(k)],
            g_send.at[k, to], g_recv.at[k, j], quarter * q4 + to,
        )

    def slab(k, step):
        ref = gbuf.at[pl.ds(quarter * q4, q4), :, near(k)]
        return remote(
            ref, ref, b_send.at[k, step + 1], b_recv.at[k, quarter], (quarter + step) * q4 + j
        )

    def l_slab(k):
        return remote(
            lbuf.at[pl.ds(0, q4), :, near(k)], lbuf.at[pl.ds(q4, q4), :, near(k)],
            lb_send.at[k], lb_recv.at[k], (quarter - 1) * q4 + j,
        )

    def p_copy(k, target):
        return remote(
            pout.at[pl.ds(target * q4, q4), :, near(k)], pslab.at[quarter, :, :, near(k)],
            p_send.at[k, target], p_recv.at[k, quarter], target * q4 + j,
        )

    def d_copy(k, to):
        return remote(
            psum.at[to, :, near(k)], pbuf.at[:, far(k, j)],
            d_send.at[k, to], d_recv.at[k, j], quarter * q4 + to,
        )

    def landed(ref, sem):
        pltpu.make_async_copy(ref, ref, sem).wait()

    for k in range(chunks):

        def spread(i, _, k=k):
            to = (j + i) % q4
            g_copy(k, to).start()
            l_copy(k, to).start()
            return 0

        lax.fori_loop(1, q4, spread, 0)

    for k in range(chunks):
        gbuf[me, :, near(k)] = gt[:, far(k, j)]

    def relay(k):
        own_copy(k).wait()

        def arrive(i, _):
            source = (j + i) % q4
            landed(gbuf.at[quarter * q4 + source, :, near(k)], g_recv.at[k, source])
            landed(lbuf.at[source, :, near(k)], l_recv.at[k, source])
            return 0

        lax.fori_loop(1, q4, arrive, 0)

        @pl.when(quarter == 0)
        def _():
            slab(k, 2).start()

        @pl.when(quarter <= 1)
        def _():
            slab(k, 1).start()

        @pl.when(quarter == 3)
        def _():
            slab(k, -1).start()
            l_slab(k).start()

    relay(0)

    load_u.wait()
    ubuf[...] = ubuf[...] * (s_ref[0].astype(F32) * 0.125)

    def u_copy():
        return pltpu.make_async_remote_copy(
            src_ref=ubuf, dst_ref=uprev, send_sem=u_send, recv_sem=u_recv,
            device_id=(me, cell + 1), device_id_type=MESH,
        )

    load_d.wait()

    def prepare(slot, ref, turn):
        for part in range(2):
            value = ref[part]
            flipped = value.T
            forward = flipped if turn else value
            backward = value if turn else flipped
            parts[slot, part, 0], parts[slot, part, 1] = split(forward)
            parts[slot, 2 + part, 0], parts[slot, 2 + part, 1] = split(backward)

    prepare(0, dbuf, False)
    if chunks > 1:
        relay(1)
    prepare(1, ubuf, False)

    @pl.when(cell < nc - 1)
    def _():
        u_copy().start()

    depth = q4 * (1 + third) * (1 - fourth)
    shifts = q4 * ((quarter + 1) * (1 - quarter // 2) + 4 * third)

    def wait_slab(k, source):
        landed(gbuf.at[pl.ds(source * q4, q4), :, near(k)], b_recv.at[k, source])

    def compute(k):
        @pl.when(quarter == 1)
        def _():
            wait_slab(k, 0)

        @pl.when(quarter == 2)
        def _():
            for source in (0, 1, 3):
                wait_slab(k, source)
            landed(lbuf.at[pl.ds(q4, q4), :, near(k)], lb_recv.at[k])

        def one_shift(w, _):
            def add(s, total):
                real, imaginary = total
                e = quarter * q4 + s - w
                lr, li = lbuf[s, 0, near(k)], lbuf[s, 1, near(k)]
                gr, gi = gbuf[e, 0, near(k)], gbuf[e, 1, near(k)]
                return real + (lr * gr - li * gi), imaginary + (lr * gi + li * gr)

            zero = jnp.zeros((rc, size), F32)
            first = jnp.maximum(w - quarter * q4, 0)
            real, imaginary = lax.fori_loop(first, depth, add, (zero, zero))
            pout[w, 0, near(k)] = imaginary
            pout[w, 1, near(k)] = -real
            return 0

        lax.fori_loop(0, shifts, one_shift, 0)

        @pl.when(quarter == 1)
        def _():
            p_copy(k, 0).start()

        @pl.when(quarter == 2)
        def _():
            for target in (0, 1, 3):
                p_copy(k, target).start()

    def combine(k):
        rows = near(k)

        @pl.when(quarter == 0)
        def _():
            landed(pslab.at[1, :, :, rows], p_recv.at[k, 1])

        @pl.when(quarter != 2)
        def _():
            landed(pslab.at[2, :, :, rows], p_recv.at[k, 2])

        def one(i, _):
            @pl.when(quarter == 0)
            def _():
                psum[i, :, rows] = pout[i, :, rows] + pslab[1, i, :, rows] + pslab[2, i, :, rows]

            @pl.when(quarter == 1)
            def _():
                psum[i, :, rows] = pout[q4 + i, :, rows] + pslab[2, i, :, rows]

            @pl.when(quarter == 2)
            def _():
                psum[i, :, rows] = pout[2 * q4 + i, :, rows]

            @pl.when(quarter == 3)
            def _():
                psum[i, :, rows] = pslab[2, i, :, rows]

            return 0

        lax.fori_loop(0, q4, one, 0)

        def spread(i, _):
            d_copy(k, (j + i) % q4).start()
            return 0

        lax.fori_loop(1, q4, spread, 0)
        pbuf[:, far(k, j)] = psum[j, :, rows]

    def neighbour_copy(k, side):
        rows = pl.ds(k * span, span)
        return pltpu.make_async_remote_copy(
            src_ref=pbuf.at[:, rows],
            dst_ref=(pnext if side == 0 else pprev).at[:, rows],
            send_sem=c_send.at[k, side],
            recv_sem=c_recv.at[k, side],
            device_id=(me, cell - 1 if side == 0 else cell + 1),
            device_id_type=MESH,
        )

    def finish(k):
        rows = pl.ds(k * span, span)

        def arrive(i, _):
            source = (j + i) % q4
            landed(pbuf.at[:, far(k, source)], d_recv.at[k, source])
            return 0

        lax.fori_loop(1, q4, arrive, 0)

        @pl.when(cell > 0)
        def _():
            neighbour_copy(k, 0).start()

        @pl.when(cell < nc - 1)
        def _():
            neighbour_copy(k, 1).start()

        pltpu.make_async_copy(pbuf.at[:, rows], pol_ref.at[:, rows], out_sem.at[k]).start()

    def pair(slot, part):
        return parts[slot, part, 0], parts[slot, part, 1]

    def right_product(slot, ref, first, last):
        rows = pl.ds(first * span, (last - first) * span)
        p_real, p_imag = split(ref[0, rows]), split(ref[1, rows])
        real = product(p_real, pair(slot, 2)) + product(p_imag, pair(slot, 3))
        imaginary = product(p_imag, pair(slot, 2)) - product(p_real, pair(slot, 3))
        mid[slot, 0, 0, rows], mid[slot, 0, 1, rows] = split(real)
        mid[slot, 1, 0, rows], mid[slot, 1, 1, rows] = split(imaginary)

    def left_product(slot):
        m_real, m_imag = (mid[slot, 0, 0], mid[slot, 0, 1]), (mid[slot, 1, 0], mid[slot, 1, 1])
        real = product(pair(slot, 0), m_real) - product(pair(slot, 1), m_imag)
        imaginary = product(pair(slot, 0), m_imag) + product(pair(slot, 1), m_real)
        return real, imaginary

    def from_neighbour(side, first, last, whole):
        @pl.when(cell < nc - 1 if side == 0 else cell > 0)
        def _():
            ref = pnext if side == 0 else pprev
            for k in range(first, last):
                landed(ref.at[:, pl.ds(k * span, span)], c_recv.at[k, side])
            right_product(side + 1, ref, first, last)
            if whole:
                real, imaginary = left_product(side + 1)
                scr_ref[0] += real
                scr_ref[1] += imaginary

    bounds = sorted({0, chunks // 2, chunks - 1, chunks})
    batches = list(zip(bounds[:-1], bounds[1:]))
    for k in range(chunks + 2):
        if k + 2 < chunks:
            relay(k + 2)
        if k < chunks:
            compute(k)
        if k == 0:

            @pl.when(cell > 0)
            def _():
                landed(uprev, u_recv)
                prepare(2, uprev, True)

        if 1 <= k <= chunks:
            combine(k - 1)
        if k >= 2:
            finish(k - 2)
        for first, last in batches[:-1]:
            if k == last + 1:
                right_product(0, pbuf, first, last)
            if k == last + 2:
                from_neighbour(0, first, last, False)
                from_neighbour(1, first, last, False)

    right_product(0, pbuf, *batches[-1])
    scr_ref[0], scr_ref[1] = left_product(0)

    @pl.when(cell % 2 == 0)
    def _():
        from_neighbour(0, *batches[-1], True)
        from_neighbour(1, *batches[-1], True)

    @pl.when(cell % 2 == 1)
    def _():
        from_neighbour(1, *batches[-1], True)
        from_neighbour(0, *batches[-1], True)

    for k in range(chunks):
        rows = pl.ds(k * span, span)

        def ended(i, _, k=k):
            to = (j + i) % q4
            g_copy(k, to).wait_send()
            l_copy(k, to).wait_send()
            d_copy(k, to).wait_send()
            return 0

        lax.fori_loop(1, q4, ended, 0)

        @pl.when(quarter == 0)
        def _(k=k):
            slab(k, 2).wait_send()

        @pl.when(quarter <= 1)
        def _(k=k):
            slab(k, 1).wait_send()

        @pl.when(quarter == 3)
        def _(k=k):
            slab(k, -1).wait_send()
            l_slab(k).wait_send()

        @pl.when(quarter == 1)
        def _(k=k):
            p_copy(k, 0).wait_send()

        @pl.when(quarter == 2)
        def _(k=k):
            for target in (0, 1, 3):
                p_copy(k, target).wait_send()

        @pl.when(cell > 0)
        def _(k=k):
            neighbour_copy(k, 0).wait_send()

        @pl.when(cell < nc - 1)
        def _(k=k):
            neighbour_copy(k, 1).wait_send()

        pltpu.make_async_copy(pbuf.at[:, rows], pol_ref.at[:, rows], out_sem.at[k]).wait()

    @pl.when(cell < nc - 1)
    def _():
        u_copy().wait_send()


def body(n, nc, g_lesser, g_greater, w_diag, w_upper, coupled):
    size = g_lesser.shape[-1]
    shape = g_lesser.shape
    q4 = n // 4
    chunks = max(1, min(8, size // (8 * q4)))
    rows = size // q4
    block = (2, size, size)
    vmem = pl.BlockSpec(memory_space=pltpu.VMEM)
    anywhere = pl.BlockSpec(memory_space=pl.ANY)
    dma = pltpu.SemaphoreType.DMA
    out = pl.pallas_call(
        functools.partial(kernel, n, nc, chunks),
        out_shape=(jax.ShapeDtypeStruct(block, F32), jax.ShapeDtypeStruct(block, F32)),
        in_specs=[pl.BlockSpec(memory_space=pltpu.SMEM)] + [anywhere] * 4,
        out_specs=(anywhere, vmem),
        scratch_shapes=[
            pltpu.VMEM(block, F32),
            pltpu.VMEM(block, F32),
            pltpu.VMEM((2 * q4, 2, rows, size), F32),
            pltpu.VMEM((n, 2, rows, size), F32),
            pltpu.VMEM((n, 2, rows, size), F32),
            pltpu.VMEM((3, q4, 2, rows, size), F32),
            pltpu.VMEM((q4, 2, rows, size), F32),
            pltpu.VMEM(block, F32),
            pltpu.VMEM(block, F32),
            pltpu.VMEM(block, F32),
            pltpu.VMEM(block, F32),
            pltpu.VMEM(block, F32),
            pltpu.VMEM(block, F32),
            pltpu.VMEM((3, 4, 2, size, size), BF16),
            pltpu.VMEM((3, 2, 2, size, size), BF16),
            dma((chunks, q4)),
            dma((chunks, q4)),
            dma((chunks, q4)),
            dma((chunks, q4)),
            dma((chunks, 4)),
            dma((chunks, 4)),
            dma((chunks,)),
            dma((chunks,)),
            dma((chunks, 4)),
            dma((chunks, 3)),
            dma((chunks, q4)),
            dma((chunks, q4)),
            dma((chunks, 2)),
            dma((chunks, 2)),
            dma(()),
            dma(()),
            dma((3,)),
            dma((chunks,)),
            dma((chunks,)),
        ],
        compiler_params=pltpu.CompilerParams(
            collective_id=0, has_side_effects=True, vmem_limit_bytes=66000000
        ),
    )(
        coupled,
        g_lesser.reshape(block),
        g_greater.reshape(block),
        w_diag.reshape(block),
        w_upper.reshape(block),
    )
    factor = 1.0 / math.sqrt(n)
    return tuple(array.reshape(shape) * factor for array in out)


def solution(mesh):
    spec = P(None, "energy", "cell", None, None)
    return jax.shard_map(
        functools.partial(body, mesh.shape["energy"], mesh.shape["cell"]),
        mesh=mesh,
        in_specs=(spec, spec, spec, spec, P("cell")),
        out_specs=(spec, spec),
        check_vma=False,
    )
```
